32 devices in a mesh: groups: 2 (over x), img: 16 (over z, y, core).
Axes of the slice: x: 2, y: 2, z: 4, core: 2. Of those that a mesh axis runs over, the one named last changes fastest.
Arguments:
- tokens: bfloat16 [64, 128, 768], P(('groups', 'img')), parts along dimension 0, may hold values from -6 to 6
- partners: int32 [64, 8], P(('groups', 'img')), parts along dimension 0, may hold values from 0 to 31, as said below
- counts: int32 [64], P(('groups', 'img')), parts along dimension 0, may hold values from 4 to 8, as said below
- gain_query: float32 [768], replicated, may hold values from 0.5 to 12
- gain_memory: float32 [768], replicated, may hold values from 0.25 to 1.75
- w_query: bfloat16 [768, 768], replicated, may hold values from -0.21875 to 0.21875
- w_key: bfloat16 [768, 768], replicated, may hold values from -0.21875 to 0.21875
- w_value: bfloat16 [768, 768], replicated, may hold values from -0.21875 to 0.21875
- w_out: bfloat16 [768, 768], replicated, may hold values from -0.21875 to 0.21875
Outputs:
- mixed: bfloat16 [64, 128, 768], P(('groups', 'img')), parts along dimension 0
The draws below stay inside these ranges and needn't reach their ends.
There are 2 independent parts, one for each index of `groups`. The reference program is written for one: setup_inputs(seed, part) draws one part's arguments, and reference() takes and returns one part's arrays. A program takes and returns all parts, laid end to end along the dimension named above; an argument that names none is the same for every part. Nothing has to cross between parts.
Inputs may be any that keep to these rules, and one draw needn't show every extreme that they name: No image is its own partner. Over the first counts[a] partners of all images a of one device (image i belongs to device i // 2), at most 1 lie with any one device, and every device reaches 1 with some device. `counts`: every device owns an image with 8 pairs.
All inputs are finite; a program needn't handle non-finite values.
Results may differ from the reference program's by a relative error of at most 0.0067.
Values may be sent and summed in bfloat16 or wider, within the bound.
A program may use at most 128 MiB of HBM per device.

```python
import jax
import jax.numpy as jnp
from jax import lax

D = 768
HEADS = 12
HEAD_DIM = 64
TOK = 128
PARTNERS = 8
IMG_DEV = 2
IMAGES = 32
CAP = 1


def scene_graph(key):
    device_count = IMAGES // IMG_DEV
    pieces = jax.random.split(jax.random.fold_in(key, 7), 6)
    pair_counts = jax.random.randint(pieces[0], (device_count, IMG_DEV), PARTNERS // 2, PARTNERS + 1)
    full_image = jax.random.randint(pieces[2], (device_count,), 0, IMG_DEV)
    pair_counts = jnp.where(jnp.arange(IMG_DEV)[None, :] == full_image[:, None], PARTNERS, pair_counts)
    live = (jnp.arange(PARTNERS)[None, None, :] < pair_counts[:, :, None]).reshape(device_count, IMG_DEV * PARTNERS)
    rank = jnp.cumsum(live.astype(jnp.int32), axis=1) - 1
    orders = jax.vmap(lambda sub: jax.random.permutation(sub, device_count))(jax.random.split(pieces[3], device_count))
    slot_owner = jnp.take_along_axis(orders, jnp.clip(rank // CAP, 0, device_count - 1), axis=1)
    other_owner = jax.random.randint(pieces[4], (device_count, IMG_DEV * PARTNERS), 0, device_count)
    owner = jnp.where(live, slot_owner, other_owner)
    within = jax.random.randint(pieces[5], (device_count, IMG_DEV * PARTNERS), 0, IMG_DEV)
    query_image = jnp.arange(device_count)[:, None] * IMG_DEV + jnp.repeat(jnp.arange(IMG_DEV), PARTNERS)[None, :]
    partner = owner * IMG_DEV + within
    partner = jnp.where(partner == query_image, owner * IMG_DEV + (within + 1) % IMG_DEV, partner)
    return (pair_counts.reshape(IMAGES).astype(jnp.int32), partner.reshape(IMAGES, PARTNERS).astype(jnp.int32))


def draw_partners(key, part):
    return scene_graph(key)[1]


def draw_counts(key, part):
    return scene_graph(key)[0]


def draw_gain_query(key, part):
    gain = jnp.exp(jax.random.uniform(key, (D,), jnp.float32, jnp.log(0.5), jnp.log(2.0)))
    return gain.astype(jnp.float32)


def level_of(own_key, dims, cuts, smallest, largest):
    def one(axis_at, blocks):
        steps = jax.random.uniform(jax.random.fold_in(jax.random.fold_in(own_key, 6), axis_at), (blocks,), jnp.float32, smallest / len(cuts), largest / len(cuts))
        return jnp.repeat(jnp.exp(steps), dims[axis_at] // blocks).reshape((-1,) + (1,) * (len(dims) - axis_at - 1))

    loudness = one(*cuts[0])
    for cut in cuts[1:]:
        loudness = loudness * one(*cut)
    return loudness


def centred(own_key, shape, width, bound, cuts=(), kind=jnp.bfloat16):
    factor_of = level_of(own_key, shape, cuts, -0.22, 0.18) if cuts else 1.0
    drawn = jax.random.normal(own_key, shape, jnp.float32) * width * factor_of
    return jnp.minimum(jnp.maximum(drawn, -bound), bound).astype(kind)


def setup_inputs(seed: int = 0, part: int = 0) -> dict:
    streams_of = jax.random.split(jax.random.key(seed), 10)
    own_keys = jax.random.split(jax.random.fold_in(streams_of[9], part), 10)
    tokens = centred(own_keys[0], (IMAGES, TOK, D), 1.0, 6.0, ((0, 16),))
    partners = draw_partners(jax.random.fold_in(jax.random.fold_in(streams_of[9], part), 71), part)
    counts = draw_counts(jax.random.fold_in(jax.random.fold_in(streams_of[9], part), 71), part)
    gain_query = draw_gain_query(jax.random.fold_in(streams_of[9], 71), part)
    gain_memory = jnp.clip(1.0 + 0.15 * jax.random.normal(streams_of[4], (D,), jnp.float32), 0.25, 1.75)
    w_query = centred(streams_of[5], (D, D), D ** -0.5, 0.21875)
    w_key = centred(streams_of[6], (D, D), D ** -0.5, 0.21875)
    w_value = centred(streams_of[7], (D, D), D ** -0.5, 0.21875)
    w_out = centred(streams_of[8], (D, D), D ** -0.5, 0.21875)
    return dict(tokens=tokens, partners=partners, counts=counts, gain_query=gain_query, gain_memory=gain_memory, w_query=w_query, w_key=w_key, w_value=w_value, w_out=w_out)


def normalize(rows, gain):
    rows = rows.astype(jnp.float32)
    center = rows - lax.optimization_barrier(jnp.mean(rows, axis=-1, keepdims=True))
    spread = lax.optimization_barrier(jnp.mean(center * center, axis=-1, keepdims=True))
    return center * lax.rsqrt(spread + 1e-06) * gain

def reference(tokens, partners, counts, gain_query, gain_memory, w_query, w_key, w_value, w_out):
    rows = tokens.reshape(IMAGES * TOK, D)
    normed_query = normalize(rows, gain_query).astype(jnp.bfloat16)
    normed_memory = normalize(rows, gain_memory).astype(jnp.bfloat16)
    queries = jnp.dot(normed_query, w_query, preferred_element_type=jnp.float32).astype(jnp.bfloat16)
    keys = jnp.dot(normed_memory, w_key, preferred_element_type=jnp.float32).astype(jnp.bfloat16)
    values = jnp.dot(normed_memory, w_value, preferred_element_type=jnp.float32).astype(jnp.bfloat16)
    queries = queries.reshape(IMAGES, TOK, HEADS, HEAD_DIM)
    keys = keys.reshape(IMAGES, TOK, HEADS, HEAD_DIM)
    values = values.reshape(IMAGES, TOK, HEADS, HEAD_DIM)
    scale = 1.0 / math_sqrt(HEAD_DIM)

    def one_image(item):
        query_rows, partner_row, count = item
        key_rows = keys[partner_row.astype(jnp.int32)].astype(jnp.float32)
        value_rows = values[partner_row.astype(jnp.int32)].astype(jnp.float32)
        scores = jnp.einsum('qhd,kjhd->hkqj', query_rows.astype(jnp.float32), key_rows) * scale
        probs = lax.optimization_barrier(jax.nn.softmax(scores, axis=-1).astype(jnp.bfloat16)).astype(jnp.float32)
        pair_context = jnp.einsum('hkqj,kjhd->kqhd', probs, value_rows)
        live = jnp.arange(PARTNERS, dtype=jnp.int32) < count
        total = lax.optimization_barrier(jnp.sum(jnp.where(live[:, None, None, None], pair_context, jnp.float32(0.0)), axis=0))
        return total.reshape(TOK, D) / count.astype(jnp.float32)
    context = lax.map(one_image, (queries, partners, counts)).astype(jnp.bfloat16)
    mixed = rows.astype(jnp.float32) + jnp.dot(context.reshape(IMAGES * TOK, D), w_out, preferred_element_type=jnp.float32)
    return mixed.astype(jnp.bfloat16).reshape(IMAGES, TOK, D)

def math_sqrt(value):
    return value ** 0.5
```

```python
import functools

import jax
import jax.numpy as jnp
from jax import lax
from jax.experimental import pallas as pl
from jax.experimental.pallas import tpu as pltpu
from jax.sharding import PartitionSpec as P

HEADS = 12
HEAD_DIM = 64
LAYERS = 4
UP, DOWN, TWIN, SIBLING = 0, 1, 2, 3


def normalize(rows, gain):
    rows = rows.astype(jnp.float32)
    center = rows - jnp.mean(rows, axis=-1, keepdims=True)
    spread = jnp.mean(center * center, axis=-1, keepdims=True)
    return center * lax.rsqrt(spread + 1e-06) * gain


def slot_table(partner_rows, count_rows, own_count, peer_count):
    width = partner_rows.shape[1]
    live = (jnp.arange(width, dtype=jnp.int32)[None, :] < count_rows[:, None]).reshape(-1)
    owner = (partner_rows // own_count).reshape(-1)
    onehot = (
        (owner[:, None] == jnp.arange(peer_count, dtype=jnp.int32)[None, :]) & live[:, None]
    ).astype(jnp.int32)
    before = jnp.cumsum(onehot, axis=0) - onehot
    slot = jnp.sum(before * onehot, axis=1)
    return (owner, slot, live)


def exchange(tokens, partners, counts, gain_query, gain_memory, w_query, w_key, w_value, w_out):
    own_count, tok_rows, width = tokens.shape
    listed = partners.shape[1]
    peer_count = lax.axis_size("img")
    slot_cap = (own_count * listed + peer_count - 1) // peer_count
    first_image = lax.axis_index("img") * own_count
    rows = tokens.reshape(own_count * tok_rows, width)
    normed_query = normalize(rows, gain_query).astype(jnp.bfloat16)
    normed_memory = normalize(rows, gain_memory).astype(jnp.bfloat16)
    queries = jnp.dot(normed_query, w_query, preferred_element_type=jnp.float32).astype(
        jnp.bfloat16
    )
    queries = queries.reshape(own_count, tok_rows, HEADS, HEAD_DIM)
    my_owner, my_slot, my_live = slot_table(partners, counts, own_count, peer_count)
    target = jnp.where(my_live, my_owner, peer_count)
    request = (
        jnp.full((peer_count, slot_cap), -1, jnp.int32)
        .at[target, my_slot]
        .set(partners.reshape(-1), mode="drop")
    )
    wanted = lax.all_to_all(request, "img", split_axis=0, concat_axis=0, tiled=True)
    used = wanted >= 0
    local_index = jnp.clip(wanted - first_image, 0, own_count - 1)
    pick = jnp.clip(my_owner, 0, peer_count - 1) * slot_cap + jnp.clip(my_slot, 0, slot_cap - 1)
    picked = normed_memory.reshape(own_count, tok_rows, width)[local_index]
    got_memory = lax.all_to_all(
        jnp.where(used[:, :, None, None], picked, jnp.zeros_like(picked)),
        "img",
        split_axis=0,
        concat_axis=0,
        tiled=True,
    )
    pair_memory = got_memory.reshape(peer_count * slot_cap, tok_rows, width)[pick].reshape(
        -1, width
    )
    pair_keys = jnp.dot(pair_memory, w_key, preferred_element_type=jnp.float32).astype(jnp.bfloat16)
    pair_values = jnp.dot(pair_memory, w_value, preferred_element_type=jnp.float32).astype(
        jnp.bfloat16
    )
    pair_keys = pair_keys.reshape(own_count, listed, tok_rows, HEADS, HEAD_DIM)
    pair_values = pair_values.reshape(own_count, listed, tok_rows, HEADS, HEAD_DIM)
    scale = 1.0 / HEAD_DIM**0.5

    def one_image(item):
        query_rows, key_rows, value_rows, count = item
        scores = (
            jnp.einsum("qhd,kjhd->hkqj", query_rows, key_rows, preferred_element_type=jnp.float32)
            * scale
        )
        probs = jax.nn.softmax(scores, axis=-1).astype(jnp.bfloat16)
        pair_context = jnp.einsum(
            "hkqj,kjhd->kqhd", probs, value_rows, preferred_element_type=jnp.float32
        )
        live = jnp.arange(listed, dtype=jnp.int32) < count
        total = jnp.sum(
            jnp.where(live[:, None, None, None], pair_context, jnp.float32(0.0)), axis=0
        )
        return total.reshape(tok_rows, width) / count.astype(jnp.float32)

    context = lax.map(one_image, (queries, pair_keys, pair_values, counts)).astype(jnp.bfloat16)
    mixed = rows.astype(jnp.float32) + jnp.dot(
        context.reshape(-1, width), w_out, preferred_element_type=jnp.float32
    )
    return mixed.astype(jnp.bfloat16).reshape(own_count, tok_rows, width)


def layer_at(step, z):
    first = (LAYERS - 1 - step) // (LAYERS - 1)
    last = step // (LAYERS - 1)
    third = step // 2 * (1 - last)
    second = 1 - first - third - last
    return (
        first * z
        + second * (1 + z % 2)
        + third * ((2 + 3 * z) % 5)
        + last * (LAYERS - 1) * (1 - z // 2)
    )


def fused_kernel(
    tokens_ref,
    partners_ref,
    counts_ref,
    gain_query_ref,
    gain_memory_ref,
    w_query_ref,
    w_key_ref,
    w_value_ref,
    w_out_ref,
    mixed_ref,
    held,
    block_q,
    w_turned,
    keys_ref,
    values_ref,
    total,
    send_sem,
    recv_sem,
):
    own_count, tok_rows, width = tokens_ref.shape
    listed = partners_ref.shape[1]
    pairs = width // 128
    me = lax.axis_index("img")
    core, y, z = me % 2, me // 2 % 2, me // 4

    def index(layer, row, lane):
        return layer * 4 + row * 2 + lane

    def to(peer):
        return {"img": peer}

    up, down = index(z + 1, y, core), index(z - 1, y, core)
    twin, sibling = index(z, 1 - y, core), index(z, y, 1 - core)

    def copy(owner, way, peer):
        return pltpu.make_async_remote_copy(
            src_ref=held.at[owner],
            dst_ref=held.at[owner],
            send_sem=send_sem.at[owner, way],
            recv_sem=recv_sem.at[owner],
            device_id=to(peer),
            device_id_type=pl.DeviceIdType.MESH,
        )

    def arrived(owner):
        copy(owner, SIBLING, sibling).wait_recv()

    barrier = pltpu.get_barrier_semaphore()

    def greet(peer):
        pl.semaphore_signal(
            barrier, inc=1, device_id=to(peer), device_id_type=pl.DeviceIdType.MESH
        )

    greet(sibling)
    greet(twin)

    @pl.when(z < LAYERS - 1)
    def _():
        greet(up)

    @pl.when(z > 0)
    def _():
        greet(down)

    rows = tokens_ref[...].reshape(own_count * tok_rows, width).astype(jnp.float32)
    center = rows - jnp.mean(rows, axis=-1, keepdims=True)
    spread = jnp.mean(center * center, axis=-1, keepdims=True)
    unit = center * lax.rsqrt(spread + 1e-06)
    held[me] = (
        (unit * gain_memory_ref[...]).astype(jnp.bfloat16).reshape(own_count, tok_rows, width)
    )

    pl.semaphore_wait(barrier, 3 + (z + LAYERS - 2) // (LAYERS - 1) - z // (LAYERS - 1))

    def pass_on(layer, act):
        owner = index(layer, y, core)
        act(owner, TWIN, twin)

        @pl.when((layer <= z) & (z < LAYERS - 1))
        def _():
            act(owner, UP, up)

        @pl.when((layer >= z) & (z > 0))
        def _():
            act(owner, DOWN, down)

        act(owner, SIBLING, sibling)

    def begin(owner, way, peer):
        copy(owner, way, peer).start()

    def finish(owner, way, peer):
        copy(owner, way, peer).wait_send()

    pass_on(z, begin)

    normed_query = (unit * gain_query_ref[...]).astype(jnp.bfloat16)
    w_turned[...] = w_query_ref[...].T
    queries = lax.dot_general(
        w_turned[...], normed_query, (((1,), (1,)), ((), ())), preferred_element_type=jnp.float32
    ).astype(jnp.bfloat16) * jnp.bfloat16(1.0 / HEAD_DIM**0.5)
    blank = jnp.zeros((HEAD_DIM, tok_rows), jnp.bfloat16)
    for image in range(own_count):
        for pair in range(pairs):
            both = queries[
                pair * 128 : (pair + 1) * 128, image * tok_rows : (image + 1) * tok_rows
            ]
            upper = jnp.concatenate([both[:HEAD_DIM], blank], axis=1)
            lower = jnp.concatenate([blank, both[HEAD_DIM:]], axis=1)
            block_q[image, pair] = jnp.concatenate([upper, lower], axis=0)
    w_turned[...] = w_value_ref[...].T
    total[...] = jnp.zeros_like(total)

    def pair_of(owner):
        which, within = jnp.int32(0), jnp.int32(0)
        weights = []
        for image in range(own_count):
            found = jnp.int32(0)
            for k in range(listed):
                partner = partners_ref[image, k]
                hit = ((partner // own_count == owner) & (k < counts_ref[image])).astype(jnp.int32)
                found = found + hit
                within = within + hit * (partner % own_count)
            which = which + image * found
            weights.append(found.astype(jnp.float32))
        return which, within, weights

    def attend(layer, row):
        owners = [index(layer, row, lane) for lane in range(2)]
        found = [pair_of(owner) for owner in owners]
        memory = jnp.concatenate(
            [
                jnp.where(within == 0, held[owner, 0], held[owner, 1])
                for owner, (_, within, _) in zip(owners, found)
            ],
            axis=0,
        )
        keys_ref[...] = jnp.dot(
            memory, w_key_ref[...], preferred_element_type=jnp.float32
        ).astype(jnp.bfloat16)
        values_ref[...] = lax.dot_general(
            w_turned[...], memory, (((1,), (1,)), ((), ())), preferred_element_type=jnp.float32
        ).astype(jnp.bfloat16)
        for lane, (which, _, weights) in enumerate(found):
            span = slice(lane * tok_rows, (lane + 1) * tok_rows)
            for pair in range(pairs):
                part = slice(pair * 128, (pair + 1) * 128)
                scores = jnp.dot(
                    keys_ref[span, part], block_q[which, pair], preferred_element_type=jnp.float32
                )
                grown = jnp.exp(scores - jnp.max(scores, axis=0, keepdims=True))
                share = 1.0 / jnp.sum(grown, axis=0, keepdims=True)
                probs = (grown * share).astype(jnp.bfloat16)
                mixed = jnp.dot(values_ref[part, span], probs, preferred_element_type=jnp.float32)
                for head in range(2):
                    inner = slice(head * HEAD_DIM, (head + 1) * HEAD_DIM)
                    outer = slice(pair * 128 + head * HEAD_DIM, pair * 128 + (head + 1) * HEAD_DIM)
                    piece = mixed[inner, head * tok_rows : (head + 1) * tok_rows]
                    for image in range(own_count):
                        total[image, outer] += piece * weights[image]

    def step(number, carry):
        layer = layer_at(number, z)
        arrived(index(layer, y, 1 - core))
        attend(layer, y)
        across = index(layer, 1 - y, core)
        arrived(across)
        begin(across, SIBLING, sibling)

        @pl.when(number < LAYERS - 1)
        def _():
            later = layer_at(number + 1, z)
            arrived(index(later, y, core))
            pass_on(later, begin)

        arrived(index(layer, 1 - y, 1 - core))
        attend(layer, 1 - y)
        return carry

    lax.fori_loop(0, LAYERS, step, 0)

    for image in range(own_count):
        context = (total[image] / counts_ref[image].astype(jnp.float32)).T.astype(jnp.bfloat16)
        added = jnp.dot(context, w_out_ref[...], preferred_element_type=jnp.float32)
        mixed_ref[image] = (tokens_ref[image].astype(jnp.float32) + added).astype(jnp.bfloat16)

    def settle(number, carry):
        layer = layer_at(number, z)
        pass_on(layer, finish)
        finish(index(layer, 1 - y, core), SIBLING, sibling)
        return carry

    lax.fori_loop(0, LAYERS, settle, 0)


def fused(tokens, partners, counts, gain_query, gain_memory, w_query, w_key, w_value, w_out):
    own_count, tok_rows, width = tokens.shape
    peer_count = lax.axis_size("img")
    vmem = pl.BlockSpec(memory_space=pltpu.VMEM)
    smem = pl.BlockSpec(memory_space=pltpu.SMEM)
    return pl.pallas_call(
        fused_kernel,
        out_shape=jax.ShapeDtypeStruct(tokens.shape, jnp.bfloat16),
        in_specs=[vmem, smem, smem] + [vmem] * 6,
        out_specs=vmem,
        scratch_shapes=[
            pltpu.VMEM((peer_count, own_count, tok_rows, width), jnp.bfloat16),
            pltpu.VMEM((own_count, width // 128, 128, 2 * tok_rows), jnp.bfloat16),
            pltpu.VMEM((width, width), jnp.bfloat16),
            pltpu.VMEM((2 * tok_rows, width), jnp.bfloat16),
            pltpu.VMEM((width, 2 * tok_rows), jnp.bfloat16),
            pltpu.VMEM((own_count, width, tok_rows), jnp.float32),
            pltpu.SemaphoreType.DMA((peer_count, 4)),
            pltpu.SemaphoreType.DMA((peer_count,)),
        ],
        compiler_params=pltpu.CompilerParams(
            collective_id=0, has_side_effects=True, vmem_limit_bytes=48 * 1024 * 1024
        ),
    )(
        tokens,
        partners,
        counts,
        gain_query.reshape(1, -1),
        gain_memory.reshape(1, -1),
        w_query,
        w_key,
        w_value,
        w_out,
    )


def shards(tokens, partners, *params):
    own_count, tok_rows, _ = tokens.shape
    gathers = lax.axis_size("img") == 4 * LAYERS and own_count * partners.shape[1] >= 4 * LAYERS
    if gathers and tok_rows == 128 and HEAD_DIM == 64 and own_count == 2:
        return fused(tokens, partners, *params)
    return exchange(tokens, partners, *params)


def solution(mesh):
    placed = (
        P(("groups", "img"), None, None),
        P(("groups", "img"), None),
        P(("groups", "img")),
        P(),
        P(),
        P(),
        P(),
        P(),
        P(),
    )
    return jax.shard_map(
        shards,
        mesh=mesh,
        in_specs=placed,
        out_specs=P(("groups", "img"), None, None),
        check_vma=False,
    )
```

```python
import functools

import jax
import jax.numpy as jnp
from jax import lax
from jax.experimental import pallas as pl
from jax.experimental.pallas import tpu as pltpu
from jax.sharding import PartitionSpec as P

HEADS = 12
HEAD_DIM = 64
LAYERS = 4
UP, DOWN, TWIN, SIBLING = 0, 1, 2, 3


def normalize(rows, gain):
    rows = rows.astype(jnp.float32)
    center = rows - jnp.mean(rows, axis=-1, keepdims=True)
    spread = jnp.mean(center * center, axis=-1, keepdims=True)
    return center * lax.rsqrt(spread + 1e-06) * gain


def slot_table(partner_rows, count_rows, own_count, peer_count):
    width = partner_rows.shape[1]
    live = (jnp.arange(width, dtype=jnp.int32)[None, :] < count_rows[:, None]).reshape(-1)
    owner = (partner_rows // own_count).reshape(-1)
    onehot = (
        (owner[:, None] == jnp.arange(peer_count, dtype=jnp.int32)[None, :]) & live[:, None]
    ).astype(jnp.int32)
    before = jnp.cumsum(onehot, axis=0) - onehot
    slot = jnp.sum(before * onehot, axis=1)
    return (owner, slot, live)


def exchange(tokens, partners, counts, gain_query, gain_memory, w_query, w_key, w_value, w_out):
    own_count, tok_rows, width = tokens.shape
    listed = partners.shape[1]
    peer_count = lax.axis_size("img")
    slot_cap = (own_count * listed + peer_count - 1) // peer_count
    first_image = lax.axis_index("img") * own_count
    rows = tokens.reshape(own_count * tok_rows, width)
    normed_query = normalize(rows, gain_query).astype(jnp.bfloat16)
    normed_memory = normalize(rows, gain_memory).astype(jnp.bfloat16)
    queries = jnp.dot(normed_query, w_query, preferred_element_type=jnp.float32).astype(
        jnp.bfloat16
    )
    queries = queries.reshape(own_count, tok_rows, HEADS, HEAD_DIM)
    my_owner, my_slot, my_live = slot_table(partners, counts, own_count, peer_count)
    target = jnp.where(my_live, my_owner, peer_count)
    request = (
        jnp.full((peer_count, slot_cap), -1, jnp.int32)
        .at[target, my_slot]
        .set(partners.reshape(-1), mode="drop")
    )
    wanted = lax.all_to_all(request, "img", split_axis=0, concat_axis=0, tiled=True)
    used = wanted >= 0
    local_index = jnp.clip(wanted - first_image, 0, own_count - 1)
    pick = jnp.clip(my_owner, 0, peer_count - 1) * slot_cap + jnp.clip(my_slot, 0, slot_cap - 1)
    picked = normed_memory.reshape(own_count, tok_rows, width)[local_index]
    got_memory = lax.all_to_all(
        jnp.where(used[:, :, None, None], picked, jnp.zeros_like(picked)),
        "img",
        split_axis=0,
        concat_axis=0,
        tiled=True,
    )
    pair_memory = got_memory.reshape(peer_count * slot_cap, tok_rows, width)[pick].reshape(
        -1, width
    )
    pair_keys = jnp.dot(pair_memory, w_key, preferred_element_type=jnp.float32).astype(jnp.bfloat16)
    pair_values = jnp.dot(pair_memory, w_value, preferred_element_type=jnp.float32).astype(
        jnp.bfloat16
    )
    pair_keys = pair_keys.reshape(own_count, listed, tok_rows, HEADS, HEAD_DIM)
    pair_values = pair_values.reshape(own_count, listed, tok_rows, HEADS, HEAD_DIM)
    scale = 1.0 / HEAD_DIM**0.5

    def one_image(item):
        query_rows, key_rows, value_rows, count = item
        scores = (
            jnp.einsum("qhd,kjhd->hkqj", query_rows, key_rows, preferred_element_type=jnp.float32)
            * scale
        )
        probs = jax.nn.softmax(scores, axis=-1).astype(jnp.bfloat16)
        pair_context = jnp.einsum(
            "hkqj,kjhd->kqhd", probs, value_rows, preferred_element_type=jnp.float32
        )
        live = jnp.arange(listed, dtype=jnp.int32) < count
        total = jnp.sum(
            jnp.where(live[:, None, None, None], pair_context, jnp.float32(0.0)), axis=0
        )
        return total.reshape(tok_rows, width) / count.astype(jnp.float32)

    context = lax.map(one_image, (queries, pair_keys, pair_values, counts)).astype(jnp.bfloat16)
    mixed = rows.astype(jnp.float32) + jnp.dot(
        context.reshape(-1, width), w_out, preferred_element_type=jnp.float32
    )
    return mixed.astype(jnp.bfloat16).reshape(own_count, tok_rows, width)


def layer_at(step, z):
    first = (LAYERS - 1 - step) // (LAYERS - 1)
    last = step // (LAYERS - 1)
    third = step // 2 * (1 - last)
    second = 1 - first - third - last
    return (
        first * z
        + second * (1 + z % 2)
        + third * ((2 + 3 * z) % 5)
        + last * (LAYERS - 1) * (1 - z // 2)
    )


def fused_kernel(
    *refs,
):
    sources, (mixed_ref,) = refs[:9], refs[9:10]
    landed, load_sem = refs[10:19], refs[19]
    (
        tokens_ref,
        partners_ref,
        counts_ref,
        gain_query_ref,
        gain_memory_ref,
        w_query_ref,
        w_key_ref,
        w_value_ref,
        w_out_ref,
    ) = landed
    held, block_q, w_turned, keys_ref, values_ref, total, send_sem, recv_sem = refs[20:]
    loads = [
        pltpu.make_async_copy(source, place, load_sem.at[number])
        for number, (source, place) in enumerate(zip(sources, landed))
    ]
    for number in (0, 4, 3, 5, 7, 6, 1, 2, 8):
        loads[number].start()
    own_count, tok_rows, width = tokens_ref.shape
    listed = partners_ref.shape[1]
    pairs = width // 128
    me = lax.axis_index("img")
    core, y, z = me % 2, me // 2 % 2, me // 4

    def index(layer, row, lane):
        return layer * 4 + row * 2 + lane

    def to(peer):
        return {"img": peer}

    up, down = index(z + 1, y, core), index(z - 1, y, core)
    twin, sibling = index(z, 1 - y, core), index(z, y, 1 - core)

    def copy(owner, way, peer):
        return pltpu.make_async_remote_copy(
            src_ref=held.at[owner],
            dst_ref=held.at[owner],
            send_sem=send_sem.at[owner, way],
            recv_sem=recv_sem.at[owner],
            device_id=to(peer),
            device_id_type=pl.DeviceIdType.MESH,
        )

    def arrived(owner):
        copy(owner, SIBLING, sibling).wait_recv()

    barrier = pltpu.get_barrier_semaphore()

    def greet(peer):
        pl.semaphore_signal(
            barrier, inc=1, device_id=to(peer), device_id_type=pl.DeviceIdType.MESH
        )

    greet(sibling)
    greet(twin)

    @pl.when(z < LAYERS - 1)
    def _():
        greet(up)

    @pl.when(z > 0)
    def _():
        greet(down)

    loads[0].wait()
    loads[4].wait()
    rows = tokens_ref[...].reshape(own_count * tok_rows, width).astype(jnp.float32)
    center = rows - jnp.mean(rows, axis=-1, keepdims=True)
    spread = jnp.mean(center * center, axis=-1, keepdims=True)
    unit = center * lax.rsqrt(spread + 1e-06)
    held[me] = (
        (unit * gain_memory_ref[...].reshape(1, width)).astype(jnp.bfloat16).reshape(own_count, tok_rows, width)
    )

    pl.semaphore_wait(barrier, 3 + (z + LAYERS - 2) // (LAYERS - 1) - z // (LAYERS - 1))

    def pass_on(layer, act):
        owner = index(layer, y, core)
        act(owner, TWIN, twin)

        @pl.when((layer <= z) & (z < LAYERS - 1))
        def _():
            act(owner, UP, up)

        @pl.when((layer >= z) & (z > 0))
        def _():
            act(owner, DOWN, down)

        act(owner, SIBLING, sibling)

    def begin(owner, way, peer):
        copy(owner, way, peer).start()

    def finish(owner, way, peer):
        copy(owner, way, peer).wait_send()

    pass_on(z, begin)

    loads[3].wait()
    loads[5].wait()
    normed_query = (unit * gain_query_ref[...].reshape(1, width)).astype(jnp.bfloat16)
    w_turned[...] = w_query_ref[...].T
    queries = lax.dot_general(
        w_turned[...], normed_query, (((1,), (1,)), ((), ())), preferred_element_type=jnp.float32
    ).astype(jnp.bfloat16) * jnp.bfloat16(1.0 / HEAD_DIM**0.5)
    blank = jnp.zeros((HEAD_DIM, tok_rows), jnp.bfloat16)
    for image in range(own_count):
        for pair in range(pairs):
            both = queries[
                pair * 128 : (pair + 1) * 128, image * tok_rows : (image + 1) * tok_rows
            ]
            upper = jnp.concatenate([both[:HEAD_DIM], blank], axis=1)
            lower = jnp.concatenate([blank, both[HEAD_DIM:]], axis=1)
            block_q[image, pair] = jnp.concatenate([upper, lower], axis=0)
    loads[7].wait()
    w_turned[...] = w_value_ref[...].T
    loads[6].wait()
    loads[1].wait()
    loads[2].wait()
    total[...] = jnp.zeros_like(total)

    def pair_of(owner):
        which, within = jnp.int32(0), jnp.int32(0)
        weights = []
        for image in range(own_count):
            found = jnp.int32(0)
            for k in range(listed):
                partner = partners_ref[image, k]
                hit = ((partner // own_count == owner) & (k < counts_ref[image])).astype(jnp.int32)
                found = found + hit
                within = within + hit * (partner % own_count)
            which = which + image * found
            weights.append(found.astype(jnp.float32))
        return which, within, weights

    def attend(layer, row):
        owners = [index(layer, row, lane) for lane in range(2)]
        found = [pair_of(owner) for owner in owners]
        memory = jnp.concatenate(
            [
                jnp.where(within == 0, held[owner, 0], held[owner, 1])
                for owner, (_, within, _) in zip(owners, found)
            ],
            axis=0,
        )
        keys_ref[...] = jnp.dot(
            memory, w_key_ref[...], preferred_element_type=jnp.float32
        ).astype(jnp.bfloat16)
        values_ref[...] = lax.dot_general(
            w_turned[...], memory, (((1,), (1,)), ((), ())), preferred_element_type=jnp.float32
        ).astype(jnp.bfloat16)
        for lane, (which, _, weights) in enumerate(found):
            span = slice(lane * tok_rows, (lane + 1) * tok_rows)
            for pair in range(pairs):
                part = slice(pair * 128, (pair + 1) * 128)
                scores = jnp.dot(
                    keys_ref[span, part], block_q[which, pair], preferred_element_type=jnp.float32
                )
                grown = jnp.exp(scores - jnp.max(scores, axis=0, keepdims=True))
                share = 1.0 / jnp.sum(grown, axis=0, keepdims=True)
                probs = (grown * share).astype(jnp.bfloat16)
                mixed = jnp.dot(values_ref[part, span], probs, preferred_element_type=jnp.float32)
                for head in range(2):
                    inner = slice(head * HEAD_DIM, (head + 1) * HEAD_DIM)
                    outer = slice(pair * 128 + head * HEAD_DIM, pair * 128 + (head + 1) * HEAD_DIM)
                    piece = mixed[inner, head * tok_rows : (head + 1) * tok_rows]
                    for image in range(own_count):
                        total[image, outer] += piece * weights[image]

    def step(number, carry):
        layer = layer_at(number, z)
        arrived(index(layer, y, 1 - core))
        attend(layer, y)
        across = index(layer, 1 - y, core)
        arrived(across)
        begin(across, SIBLING, sibling)

        @pl.when(number < LAYERS - 1)
        def _():
            later = layer_at(number + 1, z)
            arrived(index(later, y, core))
            pass_on(later, begin)

        arrived(index(layer, 1 - y, 1 - core))
        attend(layer, 1 - y)
        return carry

    lax.fori_loop(0, LAYERS, step, 0)

    loads[8].wait()
    for image in range(own_count):
        context = (total[image] / counts_ref[image].astype(jnp.float32)).T.astype(jnp.bfloat16)
        added = jnp.dot(context, w_out_ref[...], preferred_element_type=jnp.float32)
        mixed_ref[image] = (tokens_ref[image].astype(jnp.float32) + added).astype(jnp.bfloat16)

    def settle(number, carry):
        layer = layer_at(number, z)
        pass_on(layer, finish)
        finish(index(layer, 1 - y, core), SIBLING, sibling)
        return carry

    lax.fori_loop(0, LAYERS, settle, 0)


def fused(tokens, partners, counts, gain_query, gain_memory, w_query, w_key, w_value, w_out):
    own_count, tok_rows, width = tokens.shape
    peer_count = lax.axis_size("img")
    operands = (
        tokens, partners, counts, gain_query, gain_memory, w_query, w_key, w_value, w_out
    )
    spaces = [pltpu.VMEM, pltpu.SMEM, pltpu.SMEM] + [pltpu.VMEM] * 6
    return pl.pallas_call(
        fused_kernel,
        out_shape=jax.ShapeDtypeStruct(tokens.shape, jnp.bfloat16),
        in_specs=[pl.BlockSpec(memory_space=pltpu.HBM)] * len(operands),
        out_specs=pl.BlockSpec(memory_space=pltpu.VMEM),
        scratch_shapes=[space(x.shape, x.dtype) for space, x in zip(spaces, operands)]
        + [
            pltpu.SemaphoreType.DMA((len(operands),)),
            pltpu.VMEM((peer_count, own_count, tok_rows, width), jnp.bfloat16),
            pltpu.VMEM((own_count, width // 128, 128, 2 * tok_rows), jnp.bfloat16),
            pltpu.VMEM((width, width), jnp.bfloat16),
            pltpu.VMEM((2 * tok_rows, width), jnp.bfloat16),
            pltpu.VMEM((width, 2 * tok_rows), jnp.bfloat16),
            pltpu.VMEM((own_count, width, tok_rows), jnp.float32),
            pltpu.SemaphoreType.DMA((peer_count, 4)),
            pltpu.SemaphoreType.DMA((peer_count,)),
        ],
        compiler_params=pltpu.CompilerParams(
            collective_id=0, has_side_effects=True, vmem_limit_bytes=63 * 1024 * 1024
        ),
    )(*operands)


def shards(tokens, partners, *params):
    own_count, tok_rows, _ = tokens.shape
    gathers = lax.axis_size("img") == 4 * LAYERS and own_count * partners.shape[1] >= 4 * LAYERS
    if gathers and tok_rows == 128 and HEAD_DIM == 64 and own_count == 2:
        return fused(tokens, partners, *params)
    return exchange(tokens, partners, *params)


def solution(mesh):
    placed = (
        P(("groups", "img"), None, None),
        P(("groups", "img"), None),
        P(("groups", "img")),
        P(),
        P(),
        P(),
        P(),
        P(),
        P(),
    )
    return jax.shard_map(
        shards,
        mesh=mesh,
        in_specs=placed,
        out_specs=P(("groups", "img"), None, None),
        check_vma=False,
    )
```
